32 devices in a mesh: grp: 2 (over y), seq: 4 (over z), head: 4 (over x, core).
Axes of the slice: x: 2, y: 2, z: 4, core: 2. Of those that a mesh axis runs over, the one named last changes fastest.
Arguments:
- queries: bfloat16 [5120, 8192], P(('grp', 'seq'), 'head'), parts along dimension 0, may hold values from -30 to 30, as said below
- keys: bfloat16 [5120, 8192], P(('grp', 'seq'), 'head'), parts along dimension 0, may hold values from -6 to 6
- values: bfloat16 [5120, 8192], P(('grp', 'seq'), 'head'), parts along dimension 0, may hold values from -24 to 24, as said below
- gain: bfloat16 [8192], P('head'), may hold values from 0.25 to 1.75
Outputs:
- output: bfloat16 [5120, 8192], P(('grp', 'seq'), 'head'), parts along dimension 0
The draws below stay inside these ranges and needn't reach their ends.
There are 2 independent parts, one for each index of `grp`. The reference program is written for one: setup_inputs(seed, part) draws one part's arguments, and reference() takes and returns one part's arrays. A program takes and returns all parts, laid end to end along the dimension named above; an argument that names none is the same for every part. Nothing has to cross between parts.
Inputs may be any that keep to these rules, and one draw needn't show every extreme that they name: `queries`: query rows of various sizes. `values`: value features and rows of various sizes.
All inputs are finite; a program needn't handle non-finite values.
Results may differ from the reference program's by a relative error of at most 0.0051.
Values sent between devices are 32-bit elements; how exact they have to be, the bound alone decides.
No kernel may reach another device: no remote copies, remote signals or barrier semaphores. Data moves between devices by JAX's collectives and lax.ppermute only.
A program may use at most 64 MiB of HBM per device.

```python
import math
import jax
import jax.numpy as jnp
from jax import lax

HEADS = 64
HEAD_DIM = 128
TOK_DEV = 640
WIDTH = 8192
SEQLEN = 2560


def draw_queries(key, part):
    key_main, key_rows = jax.random.split(jax.random.fold_in(key, 11), 2)
    base = jnp.clip(jax.random.normal(key_main, (SEQLEN, WIDTH), jnp.float32), -6.0, 6.0)
    row_scale = jnp.exp(jax.random.uniform(key_rows, (SEQLEN, 1), jnp.float32, math.log(0.5), math.log(5.0)))
    return (base * row_scale).astype(jnp.bfloat16)


def draw_values(key, part):
    key_main, key_rows = jax.random.split(jax.random.fold_in(key, 23), 2)
    head_of_column = (jnp.arange(WIDTH) // HEAD_DIM).astype(jnp.float32)
    rise = head_of_column / max(HEADS - 1, 1)
    base = jnp.clip(jax.random.normal(key_main, (SEQLEN, WIDTH), jnp.float32), -6.0, 6.0)
    column_scale = 0.5 * jnp.exp(rise * math.log(4.0))
    row_scale = jnp.exp(jax.random.uniform(key_rows, (SEQLEN, 1), jnp.float32, math.log(0.5), math.log(2.0)))
    return (base * column_scale[None, :] * row_scale).astype(jnp.bfloat16)


def level_of(key, dims, cuts, least, top_value):
    loudness, own = 1.0, jax.random.fold_in(key, 6)
    for dim, blocks in cuts:
        draws = jnp.exp(jax.random.uniform(jax.random.fold_in(own, dim), (blocks,), jnp.float32, least / len(cuts), top_value / len(cuts)))
        loudness = loudness * jnp.repeat(draws, dims[dim] // blocks).reshape([-1 if axis == dim else 1 for axis in range(len(dims))])
    return loudness


def bell_draw(rng, shape, deviation, most, shards=(), kind=jnp.bfloat16):
    drawn = jax.random.normal(rng, shape, jnp.float32) * deviation
    if len(shards) > 0:
        drawn = level_of(rng, shape, shards, -0.22, 0.18) * drawn
    return jnp.clip(drawn, min=-most, max=most).astype(kind)


def setup_inputs(seed: int = 0, part: int = 0) -> dict:
    arg_keys = jax.random.split(jax.random.key(seed), 5)
    part_splits = jax.random.split(jax.random.fold_in(arg_keys[4], part), 5)
    return {
        "queries": draw_queries(jax.random.fold_in(jax.random.fold_in(arg_keys[4], part), 71), part),
        "keys": bell_draw(part_splits[1], (SEQLEN, WIDTH), 1.0, 6.0, ((0, 4), (1, 4))),
        "values": draw_values(jax.random.fold_in(jax.random.fold_in(arg_keys[4], part), 71), part),
        "gain": jnp.clip(1.0 + 0.15 * jax.random.normal(arg_keys[3], (WIDTH,), jnp.float32), 0.25, 1.75).astype(jnp.bfloat16),
    }


def reference(queries, keys, values, gain):
    width = queries.shape[1]
    blocks = queries.shape[0] // TOK_DEV

    def split_rows(array):
        return array.reshape(blocks, TOK_DEV, HEADS, HEAD_DIM)
    positions = jnp.arange(TOK_DEV)
    causal = positions[:, None] >= positions[None, :]
    highest = lax.Precision.HIGHEST

    def advance(carry, inputs):
        query_block, key_block, value_block = inputs
        query_float = query_block.astype(jnp.float32)
        key_float = key_block.astype(jnp.float32)
        value_float = value_block.astype(jnp.float32)
        scores = jnp.einsum('thd,shd->hts', query_float, key_float, precision=highest)
        scores = jnp.where(causal[None], scores, jnp.float32(0.0))
        rounded = lax.optimization_barrier(scores.astype(jnp.bfloat16)).astype(jnp.float32)
        intra_term = jnp.einsum('hts,she->the', rounded, value_float, precision=highest)
        prefix_low = lax.optimization_barrier(carry.astype(jnp.bfloat16)).astype(jnp.float32)
        inter_term = jnp.einsum('thd,hde->the', query_float, prefix_low, precision=highest)
        carry = carry + jnp.einsum('thd,the->hde', key_float, value_float, precision=highest)
        return (carry, intra_term + inter_term)
    initial = jnp.zeros((HEADS, HEAD_DIM, HEAD_DIM), jnp.float32)
    _, mixed = lax.scan(advance, initial, (split_rows(queries), split_rows(keys), split_rows(values)))
    mixed = mixed.reshape(-1, width)
    factor = lax.rsqrt(lax.optimization_barrier(jnp.mean(mixed * mixed, axis=1, keepdims=True)) + 1e-06)
    return (mixed * factor * gain.astype(jnp.float32)).astype(jnp.bfloat16)
```

```python
import functools

import jax
import jax.numpy as jnp
from jax import lax
from jax.experimental import pallas as pl
from jax.experimental.pallas import tpu as pltpu
from jax.sharding import PartitionSpec as P

HEAD_DIM = 128
CHUNK_HEADS = 2
LAG = 2
F32 = jnp.float32
BF16 = jnp.bfloat16
NT = ((1,), (1,))
NN = ((1,), (0,))
TN = ((0,), (0,))
VMEM = pl.BlockSpec(memory_space=pltpu.VMEM)
ANY = pl.BlockSpec(memory_space=pl.ANY)
LIMIT = 12 << 20


def dot(a, b, dims):
    return lax.dot_general(a, b, (dims, ((), ())), preferred_element_type=F32)


def head_columns(head):
    return slice(head * HEAD_DIM, (head + 1) * HEAD_DIM)


def first_state_body(k_ref, v_ref, out_ref):
    for h in range(CHUNK_HEADS):
        cols = head_columns(h)
        out_ref[h] = dot(k_ref[:, cols], v_ref[:, cols], TN)


def first_state(keys, values):
    tokens = keys.shape[0]
    block = pl.BlockSpec((tokens, CHUNK_HEADS * HEAD_DIM), lambda g: (0, 0))
    shape = (CHUNK_HEADS, HEAD_DIM, HEAD_DIM)
    return pl.pallas_call(
        first_state_body,
        grid=(1,),
        out_shape=jax.ShapeDtypeStruct(shape, F32),
        in_specs=[block, block],
        out_specs=pl.BlockSpec(shape, lambda g: (0, 0, 0)),
        compiler_params=pltpu.CompilerParams(vmem_limit_bytes=LIMIT),
        name="first_state",
    )(keys, values)


def merge_body(shards, has_received, *refs):
    *sources, out_ref = refs
    received = sources.pop(0) if has_received else None
    sources.pop()
    me = lax.axis_index("seq")
    value = sources[0][...]
    for source, shard in zip(sources[1:], shards[1:]):
        value = jnp.where(me >= shard, source[...], value)
    if has_received:
        value = value + received[...]
    out_ref[...] = value


def merge(shards, states, received, order):
    args = ([] if received is None else [received]) + states
    return pl.pallas_call(
        functools.partial(merge_body, shards, received is not None),
        out_shape=jax.ShapeDtypeStruct(states[0].shape, F32),
        in_specs=[VMEM] * len(args) + [ANY],
        out_specs=VMEM,
        compiler_params=pltpu.CompilerParams(vmem_limit_bytes=LIMIT),
        cost_estimate=pl.CostEstimate(flops=100000, bytes_accessed=10000, transcendentals=0),
        name="merge",
    )(*args, order)


def add_squares(mixed, squares):
    return mixed * mixed if squares is None else squares + mixed * mixed


def step_body(shards, chunks, intra, inter, final, has_squares, *refs):
    refs = list(refs)
    q_ref, k_ref, v_ref = refs[:3]
    refs = refs[3:]
    before = {}
    prefix = {}
    me = lax.axis_index("seq") if inter else None
    for c in inter:
        value = refs.pop(0)[...]
        for shard in range(2, shards):
            value = jnp.where(me >= shard, refs.pop(0)[...], value)
        prefix[c] = value.astype(BF16)
        for h in range(c * CHUNK_HEADS, (c + 1) * CHUNK_HEADS):
            before[h] = refs.pop(0)
    squares = refs.pop(0)[...] if has_squares else None
    refs = refs[2:]
    for c in chunks:
        state_ref = refs.pop(0)
        for h in range(CHUNK_HEADS):
            cols = head_columns(c * CHUNK_HEADS + h)
            state_ref[h] = dot(k_ref[:, cols], v_ref[:, cols], TN)
    for c in inter:
        for h in range(CHUNK_HEADS):
            head = c * CHUNK_HEADS + h
            mixed = before[head][...] + dot(q_ref[:, head_columns(head)], prefix[c][h], NN)
            refs.pop(0)[...] = mixed
            squares = add_squares(mixed, squares)
    if inter:
        if final:
            refs.pop(0)[...] = jnp.sum(squares.T, axis=0, keepdims=True)
        else:
            refs.pop(0)[...] = squares
    for head in intra:
        cols = head_columns(head)
        scores = dot(q_ref[:, cols], k_ref[:, cols], NT)
        row = lax.broadcasted_iota(jnp.int32, scores.shape, 0)
        column = lax.broadcasted_iota(jnp.int32, scores.shape, 1)
        scores = jnp.where(row >= column, scores, 0.0).astype(BF16)
        refs.pop(0)[...] = dot(scores, v_ref[:, cols], NN)


def step(shards, q, k, v, chunks, intra, inter, received, mixed, squares, order, final=False):
    tokens = q.shape[0]
    wide = jax.ShapeDtypeStruct((tokens, HEAD_DIM), F32)
    args, specs = [q, k, v], [VMEM] * 3
    for c in inter:
        came = [received[c + LAG * i] for i in range(shards - 1)]
        args += came
        args += [mixed[h] for h in range(c * CHUNK_HEADS, (c + 1) * CHUNK_HEADS)]
        specs += [VMEM] * (len(came) + CHUNK_HEADS)
    has_squares = bool(inter) and squares is not None
    if has_squares:
        args.append(squares)
        specs.append(VMEM)
    args += list(order)
    specs += [ANY] * 2
    out = [jax.ShapeDtypeStruct((CHUNK_HEADS, HEAD_DIM, HEAD_DIM), F32) for _ in chunks]
    out += [wide for _ in inter for _ in range(CHUNK_HEADS)]
    if inter:
        out.append(jax.ShapeDtypeStruct((1, tokens), F32) if final else wide)
    out += [wide for _ in intra]
    flops = 2 * tokens * HEAD_DIM * (
        HEAD_DIM * CHUNK_HEADS * (len(chunks) + len(inter)) + 2 * tokens * len(intra)
    )
    results = pl.pallas_call(
        functools.partial(step_body, shards, chunks, intra, inter, final, has_squares),
        out_shape=tuple(out),
        in_specs=specs,
        out_specs=tuple(VMEM for _ in out),
        compiler_params=pltpu.CompilerParams(vmem_limit_bytes=LIMIT),
        cost_estimate=pl.CostEstimate(flops=flops, bytes_accessed=100000, transcendentals=0),
        name="step",
    )(*args)
    results = list(results)
    states = {c: results.pop(0) for c in chunks}
    done = {}
    for c in inter:
        for h in range(c * CHUNK_HEADS, (c + 1) * CHUNK_HEADS):
            done[h] = results.pop(0)
    if inter:
        squares = results.pop(0)
    partial = {h: results.pop(0) for h in intra}
    return states, partial, done, squares


def finish_body(heads, width, *refs):
    mixed = refs[:heads]
    total_ref, gain_ref, out_ref, buf, sem = refs[heads:]
    tokens = buf.shape[0]
    factor = lax.rsqrt(total_ref[...] / width + 1e-06)
    factor = jnp.broadcast_to(factor, (HEAD_DIM, tokens)).T
    copies = []
    for c in range(heads // CHUNK_HEADS):
        for head in range(c * CHUNK_HEADS, (c + 1) * CHUNK_HEADS):
            cols = head_columns(head)
            buf[:, cols] = (mixed[head][...] * factor * gain_ref[:, cols].astype(F32)).astype(BF16)
        cols = slice(c * CHUNK_HEADS * HEAD_DIM, (c + 1) * CHUNK_HEADS * HEAD_DIM)
        copy = pltpu.make_async_copy(buf.at[:, cols], out_ref.at[:, cols], sem.at[c])
        copy.start()
        copies.append(copy)
    for copy in copies:
        copy.wait()


def finish(mixed, total, gain, width):
    heads = len(mixed)
    tokens = mixed[0].shape[0]
    return pl.pallas_call(
        functools.partial(finish_body, heads, float(width)),
        out_shape=jax.ShapeDtypeStruct((tokens, heads * HEAD_DIM), BF16),
        in_specs=[VMEM] * (heads + 2),
        out_specs=ANY,
        scratch_shapes=[
            pltpu.VMEM((tokens, heads * HEAD_DIM), BF16),
            pltpu.SemaphoreType.DMA((heads // CHUNK_HEADS,)),
        ],
        compiler_params=pltpu.CompilerParams(vmem_limit_bytes=LIMIT),
        name="finish",
    )(*mixed, total, gain)


def sum_over_heads(part, size):
    if size & (size - 1):
        return lax.psum(part, "head")
    reach = 1
    while reach < size:
        part = part + lax.ppermute(part, "head", [(i, i ^ reach) for i in range(size)])
        reach *= 2
    return part


def body(shards, head_shards, q, k, v, gain):
    heads = q.shape[1] // HEAD_DIM
    width = head_shards * q.shape[1]
    count = heads // CHUNK_HEADS
    last = count + LAG * (shards - 2)

    states = {0: first_state(k, v)}
    received = {}
    mixed = {}
    squares = None
    token = states[0]
    for s in range(last):
        senders = [i for i in range(shards - 1) if 0 <= s - LAG * i < count]
        if s == 0:
            mine = states[0]
        else:
            mine = merge(
                senders, [states[s - LAG * i] for i in senders], received.get(s - LAG), token
            )
        received[s] = lax.ppermute(mine, "seq", [(i, i + 1) for i in senders])

        chunks = list(range(1, count)) if s == 0 else []
        intra = [h for h in range(heads) if h * last // heads == s]
        inter = [c for c in range(count) if c + last - count + 2 == s]
        new_states, partial, done, squares = step(
            shards, q, k, v, chunks, intra, inter, received, mixed, squares, (mine, token)
        )
        states.update(new_states)
        mixed.update(partial)
        mixed.update(done)
        token = next(iter((*partial.values(), *done.values(), token)))
    for c in range(count - 2, count):
        _, _, done, squares = step(
            shards, q, k, v, [], [], [c], received, mixed, squares, (token, token), c == count - 1
        )
        mixed.update(done)
    total = sum_over_heads(squares, head_shards)
    return finish([mixed[h] for h in range(heads)], total, gain.reshape(1, -1), width)


def solution(mesh):
    placed = (
        P(("grp", "seq"), "head"),
        P(("grp", "seq"), "head"),
        P(("grp", "seq"), "head"),
        P("head"),
    )
    shape = dict(mesh.shape)
    return jax.shard_map(
        functools.partial(body, shape["seq"], shape["head"]),
        mesh=mesh,
        in_specs=placed,
        out_specs=P(("grp", "seq"), "head"),
        check_vma=False,
    )
```

```python
import functools

import jax
import jax.numpy as jnp
from jax import lax
from jax.experimental import pallas as pl
from jax.experimental.pallas import tpu as pltpu
from jax.sharding import PartitionSpec as P

HEAD_DIM = 128
CHUNKS = 5
INTRA = 5
AHEAD = 3
ROUND = 1
TRAIL = 2
FIRST_COST = 1000
LOAD_COST = 1000
STATES_COST = 100000000
MERGE_COST = 1000
WORK_COST = 200000000
F32 = jnp.float32
BF16 = jnp.bfloat16
NT = ((1,), (1,))
NN = ((1,), (0,))
TN = ((0,), (0,))
VMEM = pl.BlockSpec(memory_space=pltpu.VMEM)
ANY = pl.BlockSpec(memory_space=pl.ANY)
HBM = pl.BlockSpec(memory_space=pltpu.HBM)
PARAMS = pltpu.CompilerParams(vmem_limit_bytes=12 << 20)


def cost(flops):
    return pl.CostEstimate(flops=flops, bytes_accessed=1000, transcendentals=0)


def dot(a, b, dims):
    return lax.dot_general(a, b, (dims, ((), ())), preferred_element_type=F32)


def head_columns(head):
    return slice(head * HEAD_DIM, (head + 1) * HEAD_DIM)


class Layout:
    def __init__(self, heads):
        self.heads = heads
        tiles = heads * HEAD_DIM // 8
        self.chunks = min(CHUNKS, heads)
        self.edges = [8 * (tiles * c // self.chunks) for c in range(self.chunks + 1)]

    def shape(self, chunk):
        return jax.ShapeDtypeStruct((self.edges[chunk + 1] - self.edges[chunk], HEAD_DIM), F32)

    def pieces(self, head):
        low, high = head * HEAD_DIM, (head + 1) * HEAD_DIM
        found = []
        for c in range(self.chunks):
            a, b = max(low, self.edges[c]), min(high, self.edges[c + 1])
            if a < b:
                start = self.edges[c]
                found.append((c, slice(a - start, b - start), slice(a - low, b - low)))
        return found

    def heads_of(self, chunk):
        return [h for h in range(self.heads) if any(p[0] == chunk for p in self.pieces(h))]

    def complete_with(self, chunk):
        return [h for h in range(self.heads) if self.pieces(h)[-1][0] == chunk]


def put_states(layout, heads, k_ref, v_ref, outs):
    for head in heads:
        pieces = [piece for piece in layout.pieces(head) if piece[0] in outs]
        if pieces:
            state = dot(k_ref[:, head_columns(head)], v_ref[:, head_columns(head)], TN)
            for c, rows, own in pieces:
                outs[c][rows, :] = state[own, :]


def first_body(layout, k_hbm, v_hbm, out_ref, k_buf, v_buf, sems):
    wide = k_buf.shape[1]
    copies = [
        pltpu.make_async_copy(ref.at[:, :wide], buf, sems.at[at])
        for at, (ref, buf) in enumerate(((k_hbm, k_buf), (v_hbm, v_buf)))
    ]
    for copy in copies:
        copy.start()
    for copy in copies:
        copy.wait()
    put_states(layout, layout.heads_of(0), k_buf, v_buf, {0: out_ref})


def in_hbm(*arrays):
    return [pltpu.with_memory_space_constraint(array, pltpu.HBM) for array in arrays]


def first_states(layout, keys, values):
    wide = len(layout.heads_of(0)) * HEAD_DIM
    return pl.pallas_call(
        functools.partial(first_body, layout),
        out_shape=layout.shape(0),
        in_specs=[HBM, HBM],
        out_specs=VMEM,
        scratch_shapes=[
            pltpu.VMEM((keys.shape[0], wide), BF16),
            pltpu.VMEM((keys.shape[0], wide), BF16),
            pltpu.SemaphoreType.DMA((2,)),
        ],
        compiler_params=PARAMS,
        cost_estimate=cost(FIRST_COST),
        name="first",
    )(*in_hbm(keys, values))


def load_body(layout, groups, k_hbm, v_hbm, q_hbm, order_ref, k_ref, v_ref, q_ref, out_ref, sems):
    wide = k_ref.shape[1] // groups
    copies = []
    for at in range(groups):
        cols = slice(at * wide, (at + 1) * wide)
        copies += [
            pltpu.make_async_copy(src.at[:, cols], dst.at[:, cols], sems.at[2 * at + i])
            for i, (src, dst) in enumerate(((k_hbm, k_ref), (v_hbm, v_ref)))
        ]
    query = pltpu.make_async_copy(q_hbm, q_ref, sems.at[2 * groups])
    for copy in copies:
        copy.start()
    query.start()
    for copy in copies:
        copy.wait()
    put_states(layout, layout.heads_of(1), k_ref, v_ref, {1: out_ref})
    query.wait()


def load(layout, k, v, q, order):
    groups = 4
    return pl.pallas_call(
        functools.partial(load_body, layout, groups),
        out_shape=(
            jax.ShapeDtypeStruct(k.shape, k.dtype),
            jax.ShapeDtypeStruct(v.shape, v.dtype),
            jax.ShapeDtypeStruct(q.shape, q.dtype),
            layout.shape(1),
        ),
        in_specs=[HBM] * 3 + [ANY],
        out_specs=(VMEM, VMEM, VMEM, VMEM),
        scratch_shapes=[pltpu.SemaphoreType.DMA((2 * groups + 1,))],
        compiler_params=PARAMS,
        cost_estimate=cost(LOAD_COST),
        name="load",
    )(*in_hbm(k, v, q), order)


def states_body(layout, chunk, k_ref, v_ref, order_ref, out_ref):
    put_states(layout, layout.heads_of(chunk), k_ref, v_ref, {chunk: out_ref})


def states_of(layout, chunk, k, v, order):
    return pl.pallas_call(
        functools.partial(states_body, layout, chunk),
        out_shape=layout.shape(chunk),
        in_specs=[VMEM] * 2 + [ANY],
        out_specs=VMEM,
        compiler_params=PARAMS,
        cost_estimate=cost(STATES_COST),
        name="states",
    )(k, v, order)


def merge_body(state_ref, received_ref, order_ref, out_ref):
    out_ref[...] = state_ref[...] + received_ref[...]


def merge(state, received, order):
    return pl.pallas_call(
        merge_body,
        out_shape=jax.ShapeDtypeStruct(state.shape, F32),
        in_specs=[VMEM, VMEM, ANY],
        out_specs=VMEM,
        compiler_params=PARAMS,
        cost_estimate=cost(MERGE_COST),
        name="merge",
    )(state, received, order)


def work_body(layout, hops, intra, inter, has_squares, final, orders, *refs):
    refs = list(refs)
    q_ref, k_ref, v_ref, gain_ref = refs[:4]
    refs = refs[4:]
    came = {}
    for c in needed(layout, inter):
        came[c] = [refs.pop(0) for _ in range(hops)]
    before = {h: refs.pop(0) for h in inter}
    squares = refs.pop(0)[...] if has_squares else None
    refs = refs[orders:]
    me = lax.axis_index("seq") if inter else None
    for head in inter:
        parts = []
        for c, rows, _ in layout.pieces(head):
            part = 0.0
            for hop in range(hops):
                part = jnp.where(me == hop + 1, came[c][hop][rows, :], part)
            parts.append(part)
        prefix = parts[0] if len(parts) == 1 else jnp.concatenate(parts, axis=0)
        mixed = before[head][...] + dot(q_ref[:, head_columns(head)], prefix.astype(BF16), NN)
        refs.pop(0)[...] = mixed * gain_ref[:, head_columns(head)].astype(F32)
        squares = mixed * mixed if squares is None else squares + mixed * mixed
    if inter:
        refs.pop(0)[...] = jnp.sum(squares.T, axis=0, keepdims=True) if final else squares
    for head in intra:
        cols = head_columns(head)
        scores = dot(q_ref[:, cols], k_ref[:, cols], NT)
        row = lax.broadcasted_iota(jnp.int32, scores.shape, 0)
        column = lax.broadcasted_iota(jnp.int32, scores.shape, 1)
        scores = jnp.where(row >= column, scores, 0.0).astype(BF16)
        refs.pop(0)[...] = dot(scores, v_ref[:, cols], NN)


def needed(layout, heads):
    return sorted({p[0] for h in heads for p in layout.pieces(h)})


class Worker:
    def __init__(self, layout, hops, q, k, v, gain, states, received):
        self.layout, self.hops = layout, hops
        self.inputs = [q, k, v, gain]
        self.states = states
        self.mixed = {}
        self.squares = None
        self.received = received
        self.token = None

    def run(self, intra=(), inter=(), final=False):
        tokens = self.inputs[0].shape[0]
        wide = jax.ShapeDtypeStruct((tokens, HEAD_DIM), F32)
        args = list(self.inputs)
        for c in needed(self.layout, inter):
            args += [self.received[hop, c] for hop in range(self.hops)]
        args += [self.mixed[h] for h in inter]
        has_squares = bool(inter) and self.squares is not None
        args += [self.squares] if has_squares else []
        order = [self.token]
        out = [wide for _ in inter]
        if inter:
            out.append(jax.ShapeDtypeStruct((1, tokens), F32) if final else wide)
        out += [wide for _ in intra]
        results = pl.pallas_call(
            functools.partial(
                work_body,
                self.layout,
                self.hops,
                intra,
                inter,
                has_squares,
                final,
                len(order),
            ),
            out_shape=tuple(out),
            in_specs=[VMEM] * len(args) + [ANY] * len(order),
            out_specs=tuple(VMEM for _ in out),
            compiler_params=PARAMS,
            cost_estimate=cost(1000 + WORK_COST * (4 * len(intra) + len(inter))),
            name="work",
        )(*args, *order)
        results = list(results)
        self.token = results[-1]
        for h in inter:
            self.mixed[h] = results.pop(0)
        if inter:
            self.squares = results.pop(0)
        for h in intra:
            self.mixed[h] = results.pop(0)


def finish_body(heads, width, *refs):
    mixed = refs[:heads]
    total_ref, out_ref, buf, sems = refs[heads:]
    tokens = buf.shape[0]
    factor = lax.rsqrt(total_ref[...] / width + 1e-06)
    factor = jnp.broadcast_to(factor, (HEAD_DIM, tokens)).T
    count = sems.shape[0]
    copies = []
    for at in range(count):
        rows = slice(at * tokens // count, (at + 1) * tokens // count)
        for head in range(heads):
            cols = head_columns(head)
            buf[rows, cols] = (mixed[head][rows, :] * factor[rows, :]).astype(BF16)
        copy = pltpu.make_async_copy(buf.at[rows, :], out_ref.at[rows, :], sems.at[at])
        copy.start()
        copies.append(copy)
    for copy in copies:
        copy.wait()


def finish(mixed, total, width):
    heads = len(mixed)
    tokens = mixed[0].shape[0]
    return pl.pallas_call(
        functools.partial(finish_body, heads, float(width)),
        out_shape=jax.ShapeDtypeStruct((tokens, heads * HEAD_DIM), BF16),
        in_specs=[VMEM] * (heads + 1),
        out_specs=HBM,
        scratch_shapes=[
            pltpu.VMEM((tokens, heads * HEAD_DIM), BF16),
            pltpu.SemaphoreType.DMA((tokens // 64,)),
        ],
        compiler_params=PARAMS,
        name="finish",
    )(*mixed, total)


def sum_over_heads(part, size):
    if size & (size - 1):
        return lax.psum(part, "head")
    if ROUND == 1:
        others = [
            lax.ppermute(part, "head", [(i, i ^ reach) for i in range(size)])
            for reach in range(1, size)
        ]
        low, high = [part, *others][: size // 2], [part, *others][size // 2 :]
        return functools.reduce(jnp.add, low) + functools.reduce(jnp.add, high)
    reach = 1
    while reach < size:
        part = part + lax.ppermute(part, "head", [(i, i ^ reach) for i in range(size)])
        reach *= 2
    return part


def first_hop(shards, head_shards):
    pairs = []
    for shard in range(shards):
        for h in range(head_shards):
            there = (1 - shard, h) if shard < 2 else (shard, h ^ 1)
            pairs.append((shard * head_shards + h, there[0] * head_shards + there[1]))
    return pairs


def body(shards, head_shards, q, k, v, gain):
    heads = q.shape[1] // HEAD_DIM
    layout = Layout(heads)
    chunks = layout.chunks
    hops = shards - 1
    states = {0: first_states(layout, k, v)}
    received = {}

    def send(hop, chunk, value):
        if hop == 0 and head_shards % 2 == 0:
            pairs = first_hop(shards, head_shards)
            received[hop, chunk] = lax.ppermute(value, ("seq", "head"), pairs)
        else:
            received[hop, chunk] = lax.ppermute(value, "seq", [(hop, hop + 1)])

    send(0, 0, states[0])
    k, v, q, states[1] = load(layout, k, v, q, states[0])
    send(0, 1, states[1])
    worker = Worker(layout, hops, q, k, v, gain.reshape(1, -1), states, received)
    worker.token = states[1]

    def send_own(chunk):
        states[chunk] = worker.token = states_of(layout, chunk, k, v, worker.token)
        send(0, chunk, states[chunk])

    for c in range(2, min(AHEAD, chunks)):
        send_own(c)
    waves = chunks + TRAIL * max(0, hops - 2)
    left = list(range(heads))
    todo = list(range(chunks))
    for wave in range(waves):
        for hop in range(1, hops):
            c = wave - TRAIL * (hop - 1)
            if 0 <= c < chunks:
                worker.token = merge(states[c], received[hop - 1, c], worker.token)
                send(hop, c, worker.token)
        if wave + AHEAD < chunks:
            send_own(wave + AHEAD)
        quota = -(-len(left) // max(1, INTRA - wave))
        intra, left = left[:quota], left[quota:]
        inter = []
        c = wave - TRAIL * max(0, hops - 2) - 2
        if todo and todo[0] == c:
            inter = layout.complete_with(todo.pop(0))
        if intra or inter:
            worker.run(intra=intra, inter=inter)
    for c in todo:
        worker.run(inter=layout.complete_with(c), final=c == chunks - 1)
    total = sum_over_heads(worker.squares, head_shards)
    mixed = [worker.mixed[h] for h in range(heads)]
    return finish(mixed, total, head_shards * q.shape[1])


def solution(mesh):
    placed = (
        P(("grp", "seq"), "head"),
        P(("grp", "seq"), "head"),
        P(("grp", "seq"), "head"),
        P("head"),
    )
    shape = dict(mesh.shape)
    return jax.shard_map(
        functools.partial(body, shape["seq"], shape["head"]),
        mesh=mesh,
        in_specs=placed,
        out_specs=P(("grp", "seq"), "head"),
        check_vma=False,
    )
```

```python
import functools

import jax
import jax.numpy as jnp
from jax import lax
from jax.experimental import pallas as pl
from jax.experimental.pallas import tpu as pltpu
from jax.sharding import PartitionSpec as P

HEAD_DIM = 128
CHUNKS = 6
INTRA = 8
AHEAD = 3
ROUND = 1
TRAIL = 2
OWN = 5
OUT_ROWS = 64
FIRST_COST = 1000
LOAD_COST = 1000
STATES_COST = 100000000
MERGE_COST = 1000
WORK_COST = 200000000
BYTES = 1000
MIN_COST = 1000
F32 = jnp.float32
BF16 = jnp.bfloat16
NT = ((1,), (1,))
NN = ((1,), (0,))
TN = ((0,), (0,))
VMEM = pl.BlockSpec(memory_space=pltpu.VMEM)
ANY = pl.BlockSpec(memory_space=pl.ANY)
HBM = pl.BlockSpec(memory_space=pltpu.HBM)
PARAMS = pltpu.CompilerParams(vmem_limit_bytes=12 << 20)


def cost(flops):
    return pl.CostEstimate(flops=flops, bytes_accessed=BYTES, transcendentals=0)


def dot(a, b, dims):
    return lax.dot_general(a, b, (dims, ((), ())), preferred_element_type=F32)


def head_columns(head):
    return slice(head * HEAD_DIM, (head + 1) * HEAD_DIM)


class Layout:
    def __init__(self, heads):
        self.heads = heads
        tiles = heads * HEAD_DIM // 8
        self.chunks = min(CHUNKS, heads)
        most = -(-tiles // self.chunks)
        self.edges = [8 * max(0, tiles - most * (self.chunks - c)) for c in range(self.chunks + 1)]

    def shape(self, chunk):
        return jax.ShapeDtypeStruct((self.edges[chunk + 1] - self.edges[chunk], HEAD_DIM), F32)

    def pieces(self, head):
        low, high = head * HEAD_DIM, (head + 1) * HEAD_DIM
        found = []
        for c in range(self.chunks):
            a, b = max(low, self.edges[c]), min(high, self.edges[c + 1])
            if a < b:
                start = self.edges[c]
                found.append((c, slice(a - start, b - start), slice(a - low, b - low)))
        return found

    def heads_of(self, chunk):
        return [h for h in range(self.heads) if any(p[0] == chunk for p in self.pieces(h))]

    def complete_with(self, chunk):
        return [h for h in range(self.heads) if self.pieces(h)[-1][0] == chunk]


def put_states(layout, heads, k_ref, v_ref, outs):
    for head in heads:
        pieces = [piece for piece in layout.pieces(head) if piece[0] in outs]
        if pieces:
            state = dot(k_ref[:, head_columns(head)], v_ref[:, head_columns(head)], TN)
            for c, rows, own in pieces:
                outs[c][rows, :] = state[own, :]


def first_body(layout, k_hbm, v_hbm, out_ref, k_buf, v_buf, sems):
    wide = k_buf.shape[1]
    copies = [
        pltpu.make_async_copy(ref.at[:, :wide], buf, sems.at[at])
        for at, (ref, buf) in enumerate(((k_hbm, k_buf), (v_hbm, v_buf)))
    ]
    for copy in copies:
        copy.start()
    for copy in copies:
        copy.wait()
    put_states(layout, layout.heads_of(0), k_buf, v_buf, {0: out_ref})


def in_hbm(*arrays):
    return [pltpu.with_memory_space_constraint(array, pltpu.HBM) for array in arrays]


def first_states(layout, keys, values):
    wide = len(layout.heads_of(0)) * HEAD_DIM
    return pl.pallas_call(
        functools.partial(first_body, layout),
        out_shape=layout.shape(0),
        in_specs=[HBM, HBM],
        out_specs=VMEM,
        scratch_shapes=[
            pltpu.VMEM((keys.shape[0], wide), BF16),
            pltpu.VMEM((keys.shape[0], wide), BF16),
            pltpu.SemaphoreType.DMA((2,)),
        ],
        compiler_params=PARAMS,
        cost_estimate=cost(FIRST_COST),
        name="first",
    )(*in_hbm(keys, values))


def load_body(layout, groups, k_hbm, v_hbm, q_hbm, order_ref, k_ref, v_ref, q_ref, out_ref, sems):
    wide = k_ref.shape[1] // groups
    copies = []
    for at in range(groups):
        cols = slice(at * wide, (at + 1) * wide)
        copies += [
            pltpu.make_async_copy(src.at[:, cols], dst.at[:, cols], sems.at[2 * at + i])
            for i, (src, dst) in enumerate(((k_hbm, k_ref), (v_hbm, v_ref)))
        ]
    query = pltpu.make_async_copy(q_hbm, q_ref, sems.at[2 * groups])
    for copy in copies:
        copy.start()
    query.start()
    for copy in copies:
        copy.wait()
    put_states(layout, layout.heads_of(1), k_ref, v_ref, {1: out_ref})
    query.wait()


def load(layout, k, v, q, order):
    groups = 4
    return pl.pallas_call(
        functools.partial(load_body, layout, groups),
        out_shape=(
            jax.ShapeDtypeStruct(k.shape, k.dtype),
            jax.ShapeDtypeStruct(v.shape, v.dtype),
            jax.ShapeDtypeStruct(q.shape, q.dtype),
            layout.shape(1),
        ),
        in_specs=[HBM] * 3 + [ANY],
        out_specs=(VMEM, VMEM, VMEM, VMEM),
        scratch_shapes=[pltpu.SemaphoreType.DMA((2 * groups + 1,))],
        compiler_params=PARAMS,
        cost_estimate=cost(LOAD_COST),
        name="load",
    )(*in_hbm(k, v, q), order)


def states_body(layout, chunk, k_ref, v_ref, order_ref, out_ref):
    put_states(layout, layout.heads_of(chunk), k_ref, v_ref, {chunk: out_ref})


def states_of(layout, chunk, k, v, order):
    return pl.pallas_call(
        functools.partial(states_body, layout, chunk),
        out_shape=layout.shape(chunk),
        in_specs=[VMEM] * 2 + [ANY],
        out_specs=VMEM,
        compiler_params=PARAMS,
        cost_estimate=cost(STATES_COST),
        name="states",
    )(k, v, order)


def merge_body(state_ref, received_ref, order_ref, out_ref):
    out_ref[...] = state_ref[...] + received_ref[: state_ref.shape[0], :]


def padded(value, rows):
    lacking = rows - value.shape[0]
    return value if lacking == 0 else jnp.pad(value, ((0, lacking), (0, 0)))


def merge_two_body(state_ref, received_ref, late_ref, order_ref, out_ref):
    rows = out_ref.shape[0]
    onward = padded(state_ref[...] + received_ref[: state_ref.shape[0], :], rows)
    out_ref[...] = jnp.where(lax.axis_index("seq") == 2, onward, padded(late_ref[...], rows))


def merge_two(state, received, late, order):
    rows = max(state.shape[0], late.shape[0])
    return pl.pallas_call(
        merge_two_body,
        out_shape=jax.ShapeDtypeStruct((rows, HEAD_DIM), F32),
        in_specs=[VMEM] * 3 + [ANY],
        out_specs=VMEM,
        compiler_params=PARAMS,
        cost_estimate=cost(MERGE_COST),
        name="merge_two",
    )(state, received, late, order)


def merge(state, received, order):
    return pl.pallas_call(
        merge_body,
        out_shape=jax.ShapeDtypeStruct(state.shape, F32),
        in_specs=[VMEM, VMEM, ANY],
        out_specs=VMEM,
        compiler_params=PARAMS,
        cost_estimate=cost(MERGE_COST),
        name="merge",
    )(state, received, order)


def work_body(layout, hops, intra, inter, has_squares, final, orders, *refs):
    refs = list(refs)
    q_ref, k_ref, v_ref, gain_ref = refs[:4]
    refs = refs[4:]
    came = {}
    for c in needed(layout, inter):
        came[c] = [refs.pop(0) for _ in range(hops)]
    before = {h: refs.pop(0) for h in inter}
    squares = refs.pop(0)[...] if has_squares else None
    refs = refs[orders:]
    me = lax.axis_index("seq") if inter else None
    for head in inter:
        parts = []
        for c, rows, _ in layout.pieces(head):
            part = 0.0
            for hop in range(hops):
                part = jnp.where(me == hop + 1, came[c][hop][rows, :], part)
            parts.append(part)
        prefix = parts[0] if len(parts) == 1 else jnp.concatenate(parts, axis=0)
        mixed = before[head][...] + dot(q_ref[:, head_columns(head)], prefix.astype(BF16), NN)
        refs.pop(0)[...] = mixed * gain_ref[:, head_columns(head)].astype(F32)
        squares = mixed * mixed if squares is None else squares + mixed * mixed
    if inter:
        refs.pop(0)[...] = jnp.sum(squares.T, axis=0, keepdims=True) if final else squares
    tokens = q_ref.shape[0]
    cut = tokens * 3 // 5 // HEAD_DIM * HEAD_DIM
    for head in intra:
        cols = head_columns(head)
        out_ref = refs.pop(0)
        late = causal(dot(q_ref[cut:, cols], k_ref[cut:, cols], NT))
        late = dot(late, v_ref[cut:, cols], NN)
        if cut:
            scores = dot(q_ref[:, cols], k_ref[:cut, cols], NT)
            scores = jnp.concatenate([causal(scores[:cut]), scores[cut:].astype(BF16)], axis=0)
            early = dot(scores, v_ref[:cut, cols], NN)
            out_ref[:cut, :] = early[:cut]
            late = early[cut:] + late
        out_ref[cut:, :] = late


def causal(scores):
    row = lax.broadcasted_iota(jnp.int32, scores.shape, 0)
    column = lax.broadcasted_iota(jnp.int32, scores.shape, 1)
    return jnp.where(row >= column, scores, 0.0).astype(BF16)


def needed(layout, heads):
    return sorted({p[0] for h in heads for p in layout.pieces(h)})


class Worker:
    def __init__(self, layout, hops, q, k, v, gain, states, received):
        self.layout, self.hops = layout, hops
        self.inputs = [q, k, v, gain]
        self.states = states
        self.mixed = {}
        self.squares = None
        self.received = received
        self.token = None

    def run(self, intra=(), inter=(), final=False):
        tokens = self.inputs[0].shape[0]
        wide = jax.ShapeDtypeStruct((tokens, HEAD_DIM), F32)
        args = list(self.inputs)
        for c in needed(self.layout, inter):
            args += [self.received[hop, c] for hop in range(self.hops)]
        args += [self.mixed[h] for h in inter]
        has_squares = bool(inter) and self.squares is not None
        args += [self.squares] if has_squares else []
        order = [self.token]
        out = [wide for _ in inter]
        if inter:
            out.append(jax.ShapeDtypeStruct((1, tokens), F32) if final else wide)
        out += [wide for _ in intra]
        results = pl.pallas_call(
            functools.partial(
                work_body,
                self.layout,
                self.hops,
                intra,
                inter,
                has_squares,
                final,
                len(order),
            ),
            out_shape=tuple(out),
            in_specs=[VMEM] * len(args) + [ANY] * len(order),
            out_specs=tuple(VMEM for _ in out),
            compiler_params=PARAMS,
            cost_estimate=cost(MIN_COST + WORK_COST * (4 * len(intra) + len(inter))),
            name="work",
        )(*args, *order)
        results = list(results)
        self.token = results[-1]
        for h in inter:
            self.mixed[h] = results.pop(0)
        if inter:
            self.squares = results.pop(0)
        for h in intra:
            self.mixed[h] = results.pop(0)


def finish_body(heads, width, *refs):
    mixed = refs[:heads]
    total_ref, out_ref, buf, sems = refs[heads:]
    tokens = buf.shape[0]
    factor = lax.rsqrt(total_ref[...] / width + 1e-06)
    factor = jnp.broadcast_to(factor, (HEAD_DIM, tokens)).T
    count = sems.shape[0]
    copies = []
    for at in range(count):
        rows = slice(at * tokens // count, (at + 1) * tokens // count)
        for head in range(heads):
            cols = head_columns(head)
            buf[rows, cols] = (mixed[head][rows, :] * factor[rows, :]).astype(BF16)
        copy = pltpu.make_async_copy(buf.at[rows, :], out_ref.at[rows, :], sems.at[at])
        copy.start()
        copies.append(copy)
    for copy in copies:
        copy.wait()


def finish(mixed, total, width):
    heads = len(mixed)
    tokens = mixed[0].shape[0]
    return pl.pallas_call(
        functools.partial(finish_body, heads, float(width)),
        out_shape=jax.ShapeDtypeStruct((tokens, heads * HEAD_DIM), BF16),
        in_specs=[VMEM] * (heads + 1),
        out_specs=HBM,
        scratch_shapes=[
            pltpu.VMEM((tokens, heads * HEAD_DIM), BF16),
            pltpu.SemaphoreType.DMA((tokens // OUT_ROWS,)),
        ],
        compiler_params=PARAMS,
        name="finish",
    )(*mixed, total)


def sum_over_heads(part, size):
    if size & (size - 1):
        return lax.psum(part, "head")
    if ROUND == 1:
        others = [
            lax.ppermute(part, "head", [(i, i ^ reach) for i in range(size)])
            for reach in range(1, size)
        ]
        low, high = [part, *others][: size // 2], [part, *others][size // 2 :]
        return functools.reduce(jnp.add, low) + functools.reduce(jnp.add, high)
    reach = 1
    while reach < size:
        part = part + lax.ppermute(part, "head", [(i, i ^ reach) for i in range(size)])
        reach *= 2
    return part


def first_hop(shards, head_shards):
    pairs = []
    for shard in range(shards):
        for h in range(head_shards):
            there = (1 - shard, h) if shard < 2 else (shard, h ^ 1)
            pairs.append((shard * head_shards + h, there[0] * head_shards + there[1]))
    return pairs


def body(shards, head_shards, q, k, v, gain):
    heads = q.shape[1] // HEAD_DIM
    layout = Layout(heads)
    chunks = layout.chunks
    hops = shards - 1
    states = {0: first_states(layout, k, v)}
    received = {}

    def send(hop, chunk, value):
        if hop == 0 and head_shards % 2 == 0:
            pairs = first_hop(shards, head_shards)
            received[hop, chunk] = lax.ppermute(value, ("seq", "head"), pairs)
        else:
            received[hop, chunk] = lax.ppermute(value, "seq", [(hop, hop + 1)])

    send(0, 0, states[0])
    k, v, q, states[1] = load(layout, k, v, q, states[0])
    send(0, 1, states[1])
    worker = Worker(layout, hops, q, k, v, gain.reshape(1, -1), states, received)
    worker.token = states[1]

    def send_own(chunk):
        states[chunk] = worker.token = states_of(layout, chunk, k, v, worker.token)
        send(0, chunk, states[chunk])

    own = OWN if hops > 2 else chunks
    for c in range(2, min(AHEAD, chunks)):
        send_own(c)
    waves = chunks + TRAIL * max(0, hops - 2)
    left = list(range(heads))
    todo = list(range(chunks))
    for wave in range(waves):
        for hop in range(1, hops):
            c = wave - TRAIL * (hop - 1)
            if not 0 <= c < chunks:
                continue
            if hop == 2 and own + c < chunks:
                late = own + c
                states[late] = worker.token = states_of(layout, late, k, v, worker.token)
                worker.token = merge_two(states[c], received[1, c], states[late], worker.token)
                pairs = [(0, 1), (2, 3)]
                received[2, c] = received[0, late] = lax.ppermute(worker.token, "seq", pairs)
            else:
                worker.token = merge(states[c], received[hop - 1, c], worker.token)
                send(hop, c, worker.token)
        if wave + AHEAD < min(own, chunks):
            send_own(wave + AHEAD)
        quota = -(-len(left) // max(1, INTRA - wave))
        intra, left = left[:quota], left[quota:]
        inter = []
        c = wave - TRAIL * max(0, hops - 2) - 2
        if todo and todo[0] == c:
            inter = layout.complete_with(todo.pop(0))
        if intra or inter:
            worker.run(intra=intra, inter=inter)
    for c in todo:
        worker.run(inter=layout.complete_with(c), final=c == chunks - 1)
    total = sum_over_heads(worker.squares, head_shards)
    mixed = [worker.mixed[h] for h in range(heads)]
    return finish(mixed, total, head_shards * q.shape[1])


def solution(mesh):
    placed = (
        P(("grp", "seq"), "head"),
        P(("grp", "seq"), "head"),
        P(("grp", "seq"), "head"),
        P("head"),
    )
    shape = dict(mesh.shape)
    return jax.shard_map(
        functools.partial(body, shape["seq"], shape["head"]),
        mesh=mesh,
        in_specs=placed,
        out_specs=P(("grp", "seq"), "head"),
        check_vma=False,
    )
```

```python
import functools

import jax
import jax.numpy as jnp
from jax import lax
from jax.experimental import pallas as pl
from jax.experimental.pallas import tpu as pltpu
from jax.sharding import PartitionSpec as P

HEAD_DIM = 128
CHUNKS = 6
INTRA = 8
AHEAD = 3
ROUND = 1
TRAIL = 2
OWN = 5
OUT_ROWS = 64
FIRST_COST = 1000
LOAD_COST = 1000
STATES_COST = 100000000
MERGE_COST = 1000
WORK_COST = 200000000
BYTES = 1000
MIN_COST = 1000
F32 = jnp.float32
BF16 = jnp.bfloat16
NT = ((1,), (1,))
NN = ((1,), (0,))
TN = ((0,), (0,))
VMEM = pl.BlockSpec(memory_space=pltpu.VMEM)
ANY = pl.BlockSpec(memory_space=pl.ANY)
HBM = pl.BlockSpec(memory_space=pltpu.HBM)
PARAMS = pltpu.CompilerParams(vmem_limit_bytes=12 << 20)


def cost(flops):
    return pl.CostEstimate(flops=flops, bytes_accessed=BYTES, transcendentals=0)


def dot(a, b, dims):
    return lax.dot_general(a, b, (dims, ((), ())), preferred_element_type=F32)


def head_columns(head):
    return slice(head * HEAD_DIM, (head + 1) * HEAD_DIM)


class Layout:
    def __init__(self, heads):
        self.heads = heads
        tiles = heads * HEAD_DIM // 8
        self.chunks = min(CHUNKS, heads)
        most = -(-tiles // self.chunks)
        self.edges = [8 * max(0, tiles - most * (self.chunks - c)) for c in range(self.chunks + 1)]

    def shape(self, chunk):
        return jax.ShapeDtypeStruct((self.edges[chunk + 1] - self.edges[chunk], HEAD_DIM), F32)

    def pieces(self, head):
        low, high = head * HEAD_DIM, (head + 1) * HEAD_DIM
        found = []
        for c in range(self.chunks):
            a, b = max(low, self.edges[c]), min(high, self.edges[c + 1])
            if a < b:
                start = self.edges[c]
                found.append((c, slice(a - start, b - start), slice(a - low, b - low)))
        return found

    def heads_of(self, chunk):
        return [h for h in range(self.heads) if any(p[0] == chunk for p in self.pieces(h))]

    def complete_with(self, chunk):
        return [h for h in range(self.heads) if self.pieces(h)[-1][0] == chunk]


def put_states(layout, heads, k_ref, v_ref, outs):
    for head in heads:
        pieces = [piece for piece in layout.pieces(head) if piece[0] in outs]
        if pieces:
            state = dot(k_ref[:, head_columns(head)], v_ref[:, head_columns(head)], TN)
            for c, rows, own in pieces:
                outs[c][rows, :] = state[own, :]


def first_body(layout, k_hbm, v_hbm, out_ref, k_buf, v_buf, sems):
    wide = k_buf.shape[1]
    copies = [
        pltpu.make_async_copy(ref.at[:, :wide], buf, sems.at[at])
        for at, (ref, buf) in enumerate(((k_hbm, k_buf), (v_hbm, v_buf)))
    ]
    for copy in copies:
        copy.start()
    for copy in copies:
        copy.wait()
    put_states(layout, layout.heads_of(0), k_buf, v_buf, {0: out_ref})


def in_hbm(*arrays):
    return [pltpu.with_memory_space_constraint(array, pltpu.HBM) for array in arrays]


def first_states(layout, keys, values):
    wide = len(layout.heads_of(0)) * HEAD_DIM
    return pl.pallas_call(
        functools.partial(first_body, layout),
        out_shape=layout.shape(0),
        in_specs=[HBM, HBM],
        out_specs=VMEM,
        scratch_shapes=[
            pltpu.VMEM((keys.shape[0], wide), BF16),
            pltpu.VMEM((keys.shape[0], wide), BF16),
            pltpu.SemaphoreType.DMA((2,)),
        ],
        compiler_params=PARAMS,
        cost_estimate=cost(FIRST_COST),
        name="first",
    )(*in_hbm(keys, values))


def load_body(layout, groups, k_hbm, v_hbm, q_hbm, order_ref, k_ref, v_ref, q_ref, out_ref, sems):
    wide = k_ref.shape[1] // groups
    copies = []
    for at in range(groups):
        cols = slice(at * wide, (at + 1) * wide)
        copies += [
            pltpu.make_async_copy(src.at[:, cols], dst.at[:, cols], sems.at[2 * at + i])
            for i, (src, dst) in enumerate(((k_hbm, k_ref), (v_hbm, v_ref)))
        ]
    query = pltpu.make_async_copy(q_hbm, q_ref, sems.at[2 * groups])
    for copy in copies:
        copy.start()
    query.start()
    for copy in copies:
        copy.wait()
    put_states(layout, layout.heads_of(1), k_ref, v_ref, {1: out_ref})
    query.wait()


def load(layout, k, v, q, order):
    groups = 4
    return pl.pallas_call(
        functools.partial(load_body, layout, groups),
        out_shape=(
            jax.ShapeDtypeStruct(k.shape, k.dtype),
            jax.ShapeDtypeStruct(v.shape, v.dtype),
            jax.ShapeDtypeStruct(q.shape, q.dtype),
            layout.shape(1),
        ),
        in_specs=[HBM] * 3 + [ANY],
        out_specs=(VMEM, VMEM, VMEM, VMEM),
        scratch_shapes=[pltpu.SemaphoreType.DMA((2 * groups + 1,))],
        compiler_params=PARAMS,
        cost_estimate=cost(LOAD_COST),
        name="load",
    )(*in_hbm(k, v, q), order)


def states_body(layout, chunk, k_ref, v_ref, order_ref, out_ref):
    put_states(layout, layout.heads_of(chunk), k_ref, v_ref, {chunk: out_ref})


def states_of(layout, chunk, k, v, order):
    return pl.pallas_call(
        functools.partial(states_body, layout, chunk),
        out_shape=layout.shape(chunk),
        in_specs=[VMEM] * 2 + [ANY],
        out_specs=VMEM,
        compiler_params=PARAMS,
        cost_estimate=cost(STATES_COST),
        name="states",
    )(k, v, order)


def merge_body(state_ref, received_ref, order_ref, out_ref):
    out_ref[...] = state_ref[...] + received_ref[: state_ref.shape[0], :]


def padded(value, rows):
    lacking = rows - value.shape[0]
    return value if lacking == 0 else jnp.pad(value, ((0, lacking), (0, 0)))


def merge_two_body(state_ref, received_ref, late_ref, order_ref, out_ref):
    rows = out_ref.shape[0]
    onward = padded(state_ref[...] + received_ref[: state_ref.shape[0], :], rows)
    out_ref[...] = jnp.where(lax.axis_index("seq") == 2, onward, padded(late_ref[...], rows))


def merge_two(state, received, late, order):
    rows = max(state.shape[0], late.shape[0])
    return pl.pallas_call(
        merge_two_body,
        out_shape=jax.ShapeDtypeStruct((rows, HEAD_DIM), F32),
        in_specs=[VMEM] * 3 + [ANY],
        out_specs=VMEM,
        compiler_params=PARAMS,
        cost_estimate=cost(MERGE_COST),
        name="merge_two",
    )(state, received, late, order)


def merge(state, received, order):
    return pl.pallas_call(
        merge_body,
        out_shape=jax.ShapeDtypeStruct(state.shape, F32),
        in_specs=[VMEM, VMEM, ANY],
        out_specs=VMEM,
        compiler_params=PARAMS,
        cost_estimate=cost(MERGE_COST),
        name="merge",
    )(state, received, order)


def work_body(layout, hops, intra, inter, has_squares, final, orders, *refs):
    refs = list(refs)
    q_ref, k_ref, v_ref, gain_ref = refs[:4]
    refs = refs[4:]
    came = {}
    for c in needed(layout, inter):
        came[c] = [refs.pop(0) for _ in range(hops)]
    before = {h: refs.pop(0) for h in inter}
    squares = refs.pop(0)[...] if has_squares else None
    refs = refs[orders:]
    me = lax.axis_index("seq") if inter else None
    for head in inter:
        parts = []
        for c, rows, _ in layout.pieces(head):
            part = 0.0
            for hop in range(hops):
                part = jnp.where(me == hop + 1, came[c][hop][rows, :], part)
            parts.append(part)
        prefix = parts[0] if len(parts) == 1 else jnp.concatenate(parts, axis=0)
        mixed = before[head][...] + dot(q_ref[:, head_columns(head)], prefix.astype(BF16), NN)
        refs.pop(0)[...] = mixed * gain_ref[:, head_columns(head)].astype(F32)
        squares = mixed * mixed if squares is None else squares + mixed * mixed
    if inter:
        refs.pop(0)[...] = jnp.sum(squares.T, axis=0, keepdims=True) if final else squares
    tokens = q_ref.shape[0]
    cut = tokens * 3 // 5 // HEAD_DIM * HEAD_DIM
    for head in intra:
        cols = head_columns(head)
        out_ref = refs.pop(0)
        late = causal(dot(q_ref[cut:, cols], k_ref[cut:, cols], NT))
        late = dot(late, v_ref[cut:, cols], NN)
        if cut:
            scores = dot(q_ref[:, cols], k_ref[:cut, cols], NT)
            scores = jnp.concatenate([causal(scores[:cut]), scores[cut:].astype(BF16)], axis=0)
            early = dot(scores, v_ref[:cut, cols], NN)
            out_ref[:cut, :] = early[:cut]
            late = early[cut:] + late
        out_ref[cut:, :] = late


def causal(scores):
    row = lax.broadcasted_iota(jnp.int32, scores.shape, 0)
    column = lax.broadcasted_iota(jnp.int32, scores.shape, 1)
    return jnp.where(row >= column, scores, 0.0).astype(BF16)


def needed(layout, heads):
    return sorted({p[0] for h in heads for p in layout.pieces(h)})


class Worker:
    def __init__(self, layout, hops, q, k, v, gain, states, received):
        self.layout, self.hops = layout, hops
        self.inputs = [q, k, v, gain]
        self.states = states
        self.mixed = {}
        self.squares = None
        self.received = received
        self.token = None

    def run(self, intra=(), inter=(), final=False):
        tokens = self.inputs[0].shape[0]
        wide = jax.ShapeDtypeStruct((tokens, HEAD_DIM), F32)
        args = list(self.inputs)
        for c in needed(self.layout, inter):
            args += [self.received[hop, c] for hop in range(self.hops)]
        args += [self.mixed[h] for h in inter]
        has_squares = bool(inter) and self.squares is not None
        args += [self.squares] if has_squares else []
        order = [self.token]
        out = [wide for _ in inter]
        if inter:
            out.append(jax.ShapeDtypeStruct((1, tokens), F32) if final else wide)
        out += [wide for _ in intra]
        results = pl.pallas_call(
            functools.partial(
                work_body,
                self.layout,
                self.hops,
                intra,
                inter,
                has_squares,
                final,
                len(order),
            ),
            out_shape=tuple(out),
            in_specs=[VMEM] * len(args) + [ANY] * len(order),
            out_specs=tuple(VMEM for _ in out),
            compiler_params=PARAMS,
            cost_estimate=cost(MIN_COST + WORK_COST * (4 * len(intra) + len(inter))),
            name="work",
        )(*args, *order)
        results = list(results)
        self.token = results[-1]
        for h in inter:
            self.mixed[h] = results.pop(0)
        if inter:
            self.squares = results.pop(0)
        for h in intra:
            self.mixed[h] = results.pop(0)


def finish_body(heads, width, *refs):
    mixed = refs[:heads]
    total_ref, out_ref, buf, sems = refs[heads:]
    tokens = buf.shape[0]
    factor = lax.rsqrt(total_ref[...] / width + 1e-06)
    factor = jnp.broadcast_to(factor, (HEAD_DIM, tokens)).T
    count = sems.shape[0]
    copies = []
    for at in range(count):
        rows = slice(at * tokens // count, (at + 1) * tokens // count)
        for head in range(heads):
            cols = head_columns(head)
            buf[rows, cols] = (mixed[head][rows, :] * factor[rows, :]).astype(BF16)
        copy = pltpu.make_async_copy(buf.at[rows, :], out_ref.at[rows, :], sems.at[at])
        copy.start()
        copies.append(copy)
    for copy in copies:
        copy.wait()


def finish(mixed, total, width):
    heads = len(mixed)
    tokens = mixed[0].shape[0]
    return pl.pallas_call(
        functools.partial(finish_body, heads, float(width)),
        out_shape=jax.ShapeDtypeStruct((tokens, heads * HEAD_DIM), BF16),
        in_specs=[VMEM] * (heads + 1),
        out_specs=HBM,
        scratch_shapes=[
            pltpu.VMEM((tokens, heads * HEAD_DIM), BF16),
            pltpu.SemaphoreType.DMA((tokens // OUT_ROWS,)),
        ],
        compiler_params=PARAMS,
        name="finish",
    )(*mixed, total)


def sum_over_heads(part, size):
    if size & (size - 1):
        return lax.psum(part, "head")
    if ROUND == 1:
        others = [
            lax.ppermute(part, "head", [(i, i ^ reach) for i in range(size)])
            for reach in range(1, size)
        ]
        low, high = [part, *others][: size // 2], [part, *others][size // 2 :]
        return functools.reduce(jnp.add, low) + functools.reduce(jnp.add, high)
    reach = 1
    while reach < size:
        part = part + lax.ppermute(part, "head", [(i, i ^ reach) for i in range(size)])
        reach *= 2
    return part


def first_hop(shards, head_shards):
    pairs = []
    for shard in range(shards):
        for h in range(head_shards):
            there = (1 - shard, h) if shard < 2 else (shard, h ^ 1)
            pairs.append((shard * head_shards + h, there[0] * head_shards + there[1]))
    return pairs


def body(shards, head_shards, q, k, v, gain):
    heads = q.shape[1] // HEAD_DIM
    layout = Layout(heads)
    chunks = layout.chunks
    hops = shards - 1
    states = {0: first_states(layout, k, v)}
    received = {}

    def send(hop, chunk, value):
        if hop == 0 and head_shards % 2 == 0:
            pairs = first_hop(shards, head_shards)
            received[hop, chunk] = lax.ppermute(value, ("seq", "head"), pairs)
        else:
            received[hop, chunk] = lax.ppermute(value, "seq", [(hop, hop + 1)])

    send(0, 0, states[0])
    k, v, q, states[1] = load(layout, k, v, q, states[0])
    send(0, 1, states[1])
    worker = Worker(layout, hops, q, k, v, gain.reshape(1, -1), states, received)
    worker.token = states[1]

    def send_own(chunk):
        states[chunk] = worker.token = states_of(layout, chunk, k, v, worker.token)
        send(0, chunk, states[chunk])

    own = OWN if hops > 2 else chunks
    for c in range(2, min(AHEAD, chunks)):
        send_own(c)
    waves = chunks + TRAIL * max(0, hops - 2)
    left = list(range(heads))
    todo = list(range(chunks))
    for wave in range(waves):
        for hop in range(1, hops):
            c = wave - TRAIL * (hop - 1)
            if not 0 <= c < chunks:
                continue
            if hop == 2 and own + c < chunks:
                late = own + c
                states[late] = worker.token = states_of(layout, late, k, v, worker.token)
                worker.token = merge_two(states[c], received[1, c], states[late], worker.token)
                pairs = [(0, 1), (2, 3)]
                received[2, c] = received[0, late] = lax.ppermute(worker.token, "seq", pairs)
            else:
                worker.token = merge(states[c], received[hop - 1, c], worker.token)
                send(hop, c, worker.token)
        if wave + AHEAD < min(own, chunks):
            send_own(wave + AHEAD)
        rest = max(1, INTRA - wave - (1 if wave < own - 1 else 0))
        quota = 0 if wave == own - 1 else -(-len(left) // rest)
        intra, left = left[:quota], left[quota:]
        inter = []
        c = wave - TRAIL * max(0, hops - 2) - 2
        if todo and todo[0] == c:
            inter = layout.complete_with(todo.pop(0))
        if intra or inter:
            worker.run(intra=intra, inter=inter)
    for c in todo:
        worker.run(inter=layout.complete_with(c), final=c == chunks - 1)
    total = sum_over_heads(worker.squares, head_shards)
    mixed = [worker.mixed[h] for h in range(heads)]
    return finish(mixed, total, head_shards * q.shape[1])


def solution(mesh):
    placed = (
        P(("grp", "seq"), "head"),
        P(("grp", "seq"), "head"),
        P(("grp", "seq"), "head"),
        P("head"),
    )
    shape = dict(mesh.shape)
    return jax.shard_map(
        functools.partial(body, shape["seq"], shape["head"]),
        mesh=mesh,
        in_specs=placed,
        out_specs=P(("grp", "seq"), "head"),
        check_vma=False,
    )
```
